32 devices in a mesh: ia: 4 (over x, core), ja: 8 (over z, y).
Axes of the slice: x: 2, y: 2, z: 4, core: 2. Of those that a mesh axis runs over, the one named last changes fastest.
Arguments:
- star_pos: float32 [3, 32768], P(None, ('ia', 'ja')), may hold values from -6 to 6
- star_vel: float32 [3, 32768], P(None, ('ia', 'ja')), may hold values from -3 to 3
- star_acc: float32 [3, 32768], P(None, ('ia', 'ja')), may hold values from -3 to 3
- star_jerk: float32 [3, 32768], P(None, ('ia', 'ja')), may hold values from -6 to 6
- star_mass: float32 [32768], P(('ia', 'ja')), may hold values from 6.1035157e-06 to 0.00015258789
- star_level: int32 [32768], P(('ia', 'ja')), may hold values from 0 to 5, as said below
- active_index: int32 [256], P(('ia', 'ja')), may hold values from 0 to 1023, as said below
- active_count: int32 [32], P(('ia', 'ja')), may hold values from 1 to 8, as said below
Outputs:
- updated: float32 [12, 256], P(None, ('ia', 'ja'))
The draws below stay inside these ranges and needn't reach their ends.
Inputs may be any that keep to these rules, and one draw needn't show every extreme that they name: active_count[b] is the number of active stars of owner block b; some block has exactly 8, not always the same one. `active_index`: the slots of owner block b hold distinct local star numbers of that block; the first active_count[b] of them are exactly the stars of the block with star_level 3 or more, the others name inactive stars of the block. `star_level`: A star is active at this step exactly when its level is 3 or more.
All inputs are finite; a program needn't handle non-finite values.
Results may differ from the reference program's by a relative error of at most 0.0003.
Values sent between devices are 32-bit elements; how exact they have to be, the bound alone decides.
A program may use at most 64 MiB of HBM per device.

```python
import math
import jax
import jax.numpy as jnp
from jax import lax

STAR_DEV = 1024
ACT_CAP = 8
OWNERS = 32
NSTARS = 32768
SLOTS = 256


def active_plan(key):
    plan_key = jax.random.fold_in(key, 4711)
    count_key, order_key, full_key, slow_key, fast_key = jax.random.split(plan_key, 5)
    counts = jax.random.randint(count_key, (OWNERS,), 1, ACT_CAP + 1)
    fullest = jax.random.randint(full_key, (), 0, OWNERS)
    counts = counts.at[fullest].set(ACT_CAP)
    owner_keys = jax.random.split(order_key, OWNERS)
    orders = jax.vmap(lambda owner_key: jax.random.permutation(owner_key, STAR_DEV))(owner_keys)
    chosen = orders[:, :ACT_CAP].astype(jnp.int32)
    live_flags = (jnp.arange(ACT_CAP)[None, :] < counts[:, None]).astype(jnp.int32)
    owner_rows = jnp.broadcast_to(jnp.arange(OWNERS)[:, None], (OWNERS, ACT_CAP))
    flags = jnp.zeros((OWNERS, STAR_DEV), jnp.int32).at[owner_rows, chosen].set(live_flags)
    slow_levels = jax.random.randint(slow_key, (OWNERS, STAR_DEV), 0, 3)
    fast_levels = jax.random.randint(fast_key, (OWNERS, STAR_DEV), 3, 6)
    levels = jnp.where(flags == 1, fast_levels, slow_levels)
    return (chosen.reshape(-1), counts.astype(jnp.int32), levels.reshape(-1).astype(jnp.int32))


def draw_active_index(key, part):
    return active_plan(key)[0]


def draw_active_count(key, part):
    return active_plan(key)[1]


def draw_star_level(key, part):
    return active_plan(key)[2]


def level_of(own_key, extent, cuts, low, high):
    gain = 1.0
    for position, shards_of in cuts:
        heights = jax.random.uniform(jax.random.fold_in(jax.random.fold_in(own_key, 6), position), (shards_of,), jnp.float32, low / len(cuts), high / len(cuts))
        gain = gain * jnp.repeat(jnp.exp(heights), extent[position] // shards_of).reshape((-1,) + (1,) * (len(extent) - 1 - position))
    return gain


def normal_values(key, dims, spread, most, cuts=(), held_as=jnp.bfloat16):
    result = jax.random.normal(key, dims, jnp.float32) * spread
    if len(cuts) > 0:
        result = level_of(key, dims, cuts, -0.22, 0.18) * result
    return jnp.clip(result, min=-most, max=most).astype(held_as)


def setup_inputs(seed: int = 0) -> dict:
    arg_keys = jax.random.split(jax.random.key(seed), 9)
    return {
        "star_pos": normal_values(arg_keys[0], (3, NSTARS), 1.0, 6.0, ((1, 32),), jnp.float32),
        "star_vel": normal_values(arg_keys[1], (3, NSTARS), 0.5, 3.0, ((1, 32),), jnp.float32),
        "star_acc": normal_values(arg_keys[2], (3, NSTARS), 0.5, 3.0, ((1, 32),), jnp.float32),
        "star_jerk": normal_values(arg_keys[3], (3, NSTARS), 1.0, 6.0, ((1, 32),), jnp.float32),
        "star_mass": jnp.clip(jnp.exp(math.log(0.00015258789) - 3.218876 * jax.random.uniform(arg_keys[4], (NSTARS,), jnp.float32) ** level_of(arg_keys[4], (NSTARS,), ((0, 32),), -0.2, 0.2)), 6.10351571594947e-06, 0.00015258789),
        "star_level": draw_star_level(jax.random.fold_in(arg_keys[8], 71), 0),
        "active_index": draw_active_index(jax.random.fold_in(arg_keys[8], 71), 0),
        "active_count": draw_active_count(jax.random.fold_in(arg_keys[8], 71), 0),
    }


tick_now = 44
top_level = 5
tick_length = 0.125
soft_square = 0.0001

def star_age(levels):
    periods = jnp.left_shift(jnp.ones_like(levels), top_level - levels)
    remains = jnp.remainder(jnp.full_like(levels, tick_now), periods)
    ticks = jnp.where(remains == 0, periods, remains)
    return ticks.astype(jnp.float32) * tick_length

def predict(positions, velocity, accelerations, jerk_rates, star_ages):
    elapsed = star_ages[None, :]
    new_pos = positions + elapsed * (velocity + elapsed * (accelerations * 0.5 + elapsed * jerk_rates / 6.0))
    new_vel = velocity + elapsed * (accelerations + elapsed * jerk_rates * 0.5)
    return (new_pos, new_vel)

def pair_block(targets, sources):
    delta_pos = [sources[axis_num][None, :] - targets[axis_num][:, None] for axis_num in range(3)]
    delta_vel = [sources[3 + axis_num][None, :] - targets[3 + axis_num][:, None] for axis_num in range(3)]
    squared = delta_pos[0] * delta_pos[0] + delta_pos[1] * delta_pos[1] + delta_pos[2] * delta_pos[2] + soft_square
    inverse = lax.rsqrt(squared)
    inverse_sq = inverse * inverse
    strength = sources[6][None, :] * inverse * inverse_sq
    radial = 3.0 * (delta_pos[0] * delta_vel[0] + delta_pos[1] * delta_vel[1] + delta_pos[2] * delta_vel[2]) * inverse_sq
    results = [lax.optimization_barrier(jnp.sum(strength * delta_pos[axis_num], axis=1)) for axis_num in range(3)]
    results = results + [lax.optimization_barrier(jnp.sum(strength * (delta_vel[axis_num] - radial * delta_pos[axis_num]), axis=1)) for axis_num in range(3)]
    return jnp.stack(results)

def correct(targets, forces, old_acc, old_jerk, step_sizes, live_mask):
    new_acc = forces[:3]
    new_jerk = forces[3:]
    elapsed = step_sizes[None, :]
    change = old_acc - new_acc
    snap_part = -6.0 * change - elapsed * (4.0 * old_jerk + 2.0 * new_jerk)
    crackle_part = 12.0 * change + 6.0 * elapsed * (old_jerk + new_jerk)
    cor_pos = targets[:3] + elapsed * elapsed * (snap_part / 24.0 + crackle_part / 120.0)
    cor_vel = targets[3:] + elapsed * (snap_part / 6.0 + crackle_part / 24.0)
    stacked = jnp.concatenate([cor_pos, cor_vel, new_acc, new_jerk], 0)
    return jnp.where(live_mask[None, :], stacked, 0.0)

def reference(star_pos, star_vel, star_acc, star_jerk, star_mass, star_level, active_index, active_count):
    star_ages = star_age(star_level)
    pred_pos, pred_vel = predict(star_pos, star_vel, star_acc, star_jerk, star_ages)
    slot_ids = jnp.arange(SLOTS, dtype=jnp.int32)
    owner_ids = slot_ids // ACT_CAP
    chosen = (owner_ids * STAR_DEV + active_index).astype(jnp.int32)
    live_mask = slot_ids % ACT_CAP < active_count[owner_ids]
    targets = jnp.concatenate([pred_pos[:, chosen], pred_vel[:, chosen]], 0)
    sources = jnp.concatenate([pred_pos, pred_vel, star_mass[None, :]], 0)
    tile_rows = math.gcd(SLOTS, 64)
    tile_cols = math.gcd(NSTARS, 8192)
    tiles = jnp.transpose(targets.reshape(6, SLOTS // tile_rows, tile_rows), (1, 0, 2))
    source_blocks = jnp.transpose(sources.reshape(7, NSTARS // tile_cols, tile_cols), (1, 0, 2))

    def one_tile(target_tile):

        def advance(running, source_part):
            return (running + pair_block(target_tile, source_part), None)
        totals, unused = lax.scan(advance, jnp.zeros((6, tile_rows), jnp.float32), source_blocks)
        return totals
    forces = jnp.transpose(lax.map(one_tile, tiles), (1, 0, 2)).reshape(6, SLOTS)
    return correct(targets, forces, star_acc[:, chosen], star_jerk[:, chosen], star_ages[chosen], live_mask)
```

```python
import functools

import jax
import jax.numpy as jnp
from jax import lax
from jax.experimental import pallas as pl
from jax.experimental.pallas import tpu as pltpu
from jax.sharding import PartitionSpec as P

tick_now = 44
top_level = 5
tick_length = 0.125
soft_square = 0.0001

LANES = 128
SOURCE_PARTS = 2


def kernel(
    shape, pos_hbm, vel_hbm, acc_hbm, jerk_hbm, mass_hbm, level_hbm, idx_hbm, cnt_hbm, out_ref,
    pos, vel, acc, jerk, mass, level, idx, cnt, src, tgt, sums, part, got,
    in_sem, src_send, src_recv, tgt_send, tgt_recv, red_send, red_recv,
):
    n_ia, n_ja, s = shape
    n_lo = n_ja // s
    t = n_ia * n_lo
    stars = pos.shape[1]
    cap = idx.shape[0]
    ia, ja = lax.axis_index("ia"), lax.axis_index("ja")
    hi, lo = ja // n_lo, ja % n_lo
    me = ia * n_lo + lo

    def t_device(k):
        other = (me + k) % t
        return (other // n_lo, hi * n_lo + other % n_lo)

    def s_device(j):
        return (ia, ((hi + j) % s) * n_lo + lo)

    def src_copy(j):
        return pltpu.make_async_remote_copy(
            src_ref=src.at[0], dst_ref=src.at[j], send_sem=src_send.at[j],
            recv_sem=src_recv.at[j], device_id=s_device(j),
            device_id_type=pl.DeviceIdType.MESH)

    def tgt_copy(k):
        return pltpu.make_async_remote_copy(
            src_ref=tgt.at[0], dst_ref=tgt.at[k], send_sem=tgt_send.at[k],
            recv_sem=tgt_recv.at[k], device_id=t_device(k),
            device_id_type=pl.DeviceIdType.MESH)

    def red_copy(k):
        return pltpu.make_async_remote_copy(
            src_ref=part.at[k], dst_ref=got.at[k], send_sem=red_send.at[k],
            recv_sem=red_recv.at[k], device_id=t_device(t - k),
            device_id_type=pl.DeviceIdType.MESH)

    def each(low, high, body):
        def step(k, carry):
            body(k)
            return carry
        lax.fori_loop(low, high, step, 0)

    barrier = pltpu.get_barrier_semaphore()

    def greet(device):
        pl.semaphore_signal(barrier, inc=1, device_id=device,
                            device_id_type=pl.DeviceIdType.MESH)

    loads = [
        pltpu.make_async_copy(a, b, in_sem.at[i])
        for i, (a, b) in enumerate(
            [(level_hbm, level), (pos_hbm, pos), (vel_hbm, vel), (acc_hbm, acc),
             (jerk_hbm, jerk), (mass_hbm, mass), (idx_hbm, idx), (cnt_hbm, cnt)])
    ]
    for load in loads:
        load.start()
    each(1, t, lambda k: greet(t_device(k)))
    each(1, s, lambda j: greet(s_device(j)))
    for load in loads:
        load.wait()

    periods = jnp.left_shift(jnp.ones((1, stars), jnp.int32), top_level - level[...])
    remains = jnp.bitwise_and(tick_now, periods - 1)
    age = jnp.where(remains == 0, periods, remains).astype(jnp.float32) * tick_length
    pred_pos = pos[...] + age * (
        vel[...] + age * (acc[...] * 0.5 + age * jerk[...] * (1.0 / 6.0)))
    pred_vel = vel[...] + age * (acc[...] + age * jerk[...] * 0.5)
    src[0, 0:3] = pred_pos
    src[0, 3:6] = pred_vel
    src[0, 6:7] = mass[...]
    src[0, 7:8] = age

    pl.semaphore_wait(barrier, t + s - 2)
    each(1, s, lambda j: src_copy(j).start())

    slot = lax.broadcasted_iota(jnp.int32, (cap, stars), 0)
    want = jnp.zeros((cap, stars), jnp.int32)
    for i in range(cap):
        want = jnp.where(slot == i, idx[i], want)
    mask = lax.broadcasted_iota(jnp.int32, (cap, stars), 1) == want

    def pick(row):
        return jnp.sum(jnp.where(mask, row, 0.0), axis=1, keepdims=True)

    lane = lax.broadcasted_iota(jnp.int32, (cap, LANES), 1)

    def columns(values):
        tile = jnp.zeros((cap, LANES), jnp.float32)
        for i, value in enumerate(values):
            tile = jnp.where(lane == i, value, tile)
        return tile

    own = [pick(src[0, q:q + 1]) for q in range(6)]
    tgt[0] = columns(own)
    each(1, t, lambda k: tgt_copy(k).start())

    def pairs(k, j, totals):
        tile = tgt[k]
        target = [jnp.broadcast_to(tile[:, q:q + 1], (cap, LANES)) for q in range(6)]
        totals = list(totals)
        for c in range(stars // LANES):
            row = [src[j, q:q + 1, c * LANES:(c + 1) * LANES] for q in range(7)]
            d = [row[q] - target[q] for q in range(3)]
            w = [row[3 + q] - target[3 + q] for q in range(3)]
            u = lax.rsqrt(d[0] * d[0] + d[1] * d[1] + d[2] * d[2] + soft_square)
            u2 = u * u
            m = row[6] * u * u2
            r = 3.0 * (d[0] * w[0] + d[1] * w[1] + d[2] * w[2]) * u2
            for q in range(3):
                totals[q] = totals[q] + m * d[q]
                totals[3 + q] = totals[3 + q] + m * (w[q] - r * d[q])
        return totals

    zeros = [jnp.zeros((cap, LANES), jnp.float32)] * 6

    def near(k):
        totals = pairs(k, 0, zeros)
        for q in range(6):
            sums[k, q] = totals[q]

    def far(k, j_low):
        totals = [sums[k, q] for q in range(6)]
        totals = lax.fori_loop(
            j_low, s, lambda j, carry: tuple(pairs(k, j, carry)), tuple(totals))
        part[k] = columns([jnp.sum(x, axis=1, keepdims=True) for x in totals])

    near(0)
    old = [pick(acc[q:q + 1, :]) for q in range(3)] + [pick(jerk[q:q + 1, :]) for q in range(3)]
    h = pick(src[0, 7:8])

    def near_step(k):
        tgt_copy(k).wait_recv()
        near(k)

    each(1, t, near_step)
    each(1, s, lambda j: src_copy(j).wait_recv())

    def far_step(k):
        far(k, 1)
        red_copy(k).start()

    each(1, t, far_step)
    far(0, 1)

    def collect(k, total):
        red_copy(k).wait_recv()
        return total + got[k]

    total = lax.fori_loop(1, t, collect, part[0])
    force = [total[:, q:q + 1] for q in range(6)]
    rows = [None] * 12
    for q in range(3):
        new_acc, new_jerk = force[q], force[3 + q]
        change = old[q] - new_acc
        snap = -6.0 * change - h * (4.0 * old[3 + q] + 2.0 * new_jerk)
        crackle = 12.0 * change + 6.0 * h * (old[3 + q] + new_jerk)
        rows[q] = own[q] + h * h * (snap * (1.0 / 24.0) + crackle * (1.0 / 120.0))
        rows[3 + q] = own[3 + q] + h * (snap * (1.0 / 6.0) + crackle * (1.0 / 24.0))
        rows[6 + q] = new_acc
        rows[9 + q] = new_jerk
    live = lax.broadcasted_iota(jnp.int32, (cap, LANES), 0) < cnt[0]
    result = jnp.where(live, columns(rows), 0.0)
    out_ref[...] = result[:, :12]

    def drain(k):
        tgt_copy(k).wait_send()
        red_copy(k).wait_send()

    each(1, t, drain)
    each(1, s, lambda j: src_copy(j).wait_send())


def on_device(shape, star_pos, star_vel, star_acc, star_jerk, star_mass, star_level,
              active_index, active_count):
    n_ia, n_ja, s = shape
    t = n_ia * (n_ja // s)
    stars = star_mass.shape[0]
    cap = active_index.shape[0]
    f32 = jnp.float32
    return pl.pallas_call(
        functools.partial(kernel, shape),
        out_shape=jax.ShapeDtypeStruct((cap, 12), f32),
        in_specs=[pl.BlockSpec(memory_space=pltpu.HBM)] * 8,
        out_specs=pl.BlockSpec(memory_space=pltpu.VMEM),
        scratch_shapes=[
            pltpu.VMEM((3, stars), f32), pltpu.VMEM((3, stars), f32),
            pltpu.VMEM((3, stars), f32), pltpu.VMEM((3, stars), f32),
            pltpu.VMEM((1, stars), f32), pltpu.VMEM((1, stars), jnp.int32),
            pltpu.SMEM((cap,), jnp.int32), pltpu.SMEM((1,), jnp.int32),
            pltpu.VMEM((s, 8, stars), f32),
            pltpu.VMEM((t, cap, LANES), f32),
            pltpu.VMEM((t, 6, cap, LANES), f32),
            pltpu.VMEM((t, cap, LANES), f32),
            pltpu.VMEM((t, cap, LANES), f32),
            pltpu.SemaphoreType.DMA((8,)),
            pltpu.SemaphoreType.DMA((s,)), pltpu.SemaphoreType.DMA((s,)),
            pltpu.SemaphoreType.DMA((t,)), pltpu.SemaphoreType.DMA((t,)),
            pltpu.SemaphoreType.DMA((t,)), pltpu.SemaphoreType.DMA((t,)),
        ],
        compiler_params=pltpu.CompilerParams(collective_id=0, has_side_effects=True),
    )(star_pos, star_vel, star_acc, star_jerk, star_mass.reshape(1, stars),
      star_level.reshape(1, stars), active_index, active_count).T


def solution(mesh):
    n_ia, n_ja = mesh.shape["ia"], mesh.shape["ja"]
    s = SOURCE_PARTS if n_ja % SOURCE_PARTS == 0 else 1
    columns = P(None, ("ia", "ja"))
    flat = P(("ia", "ja"))
    return jax.shard_map(
        functools.partial(on_device, (n_ia, n_ja, s)), mesh=mesh,
        in_specs=(columns,) * 4 + (flat,) * 4, out_specs=columns, check_vma=False)
```

```python
import functools

import jax
import jax.numpy as jnp
from jax import lax
from jax.experimental import pallas as pl
from jax.experimental.pallas import tpu as pltpu
from jax.sharding import PartitionSpec as P

tick_now = 44
top_level = 5
tick_length = 0.125
soft_square = 0.0001

LANES = 128
SOURCE_PARTS = 4
NEAR = 2


def kernel(
    shape, pos_hbm, vel_hbm, acc_hbm, jerk_hbm, mass_hbm, level_hbm, idx_hbm, cnt_hbm, out_ref,
    pos, vel, acc, jerk, mass, level, idx, cnt, src, tgt, sums, part, got,
    in_sem, src_send, src_recv, tgt_send, tgt_recv, red_send, red_recv, ready,
):
    n_ia, n_ja, s = shape
    n_lo = n_ja // s
    t = n_ia * n_lo
    stars = pos.shape[1]
    cap = idx.shape[0]
    ia, ja = lax.axis_index("ia"), lax.axis_index("ja")
    hi, lo = ja // n_lo, ja % n_lo

    def t_device(k, sign=1):
        a, b = k // n_lo, k % n_lo
        return ((ia + sign * a + n_ia) % n_ia, hi * n_lo + (lo + sign * b + n_lo) % n_lo)

    def nearest(o):
        up = o + jnp.where(o >= hi, 1, 0)
        down = s - 1 - o - jnp.where(o >= s - 1 - hi, 1, 0)
        return jnp.where(2 * hi < s, up, down)

    def src_copy(o):
        place = nearest(o)
        return pltpu.make_async_remote_copy(
            src_ref=src.at[hi], dst_ref=src.at[hi], send_sem=src_send.at[place],
            recv_sem=src_recv.at[hi], device_id=(ia, place * n_lo + lo),
            device_id_type=pl.DeviceIdType.MESH)

    def src_arrival(o):
        place = nearest(o)
        return pltpu.make_async_remote_copy(
            src_ref=src.at[place], dst_ref=src.at[place], send_sem=src_send.at[place],
            recv_sem=src_recv.at[place], device_id=(ia, place * n_lo + lo),
            device_id_type=pl.DeviceIdType.MESH)

    def tgt_copy(k):
        return pltpu.make_async_remote_copy(
            src_ref=tgt.at[0], dst_ref=tgt.at[k], send_sem=tgt_send.at[k],
            recv_sem=tgt_recv.at[k], device_id=t_device(k),
            device_id_type=pl.DeviceIdType.MESH)

    def red_copy(k):
        return pltpu.make_async_remote_copy(
            src_ref=part.at[k], dst_ref=got.at[k], send_sem=red_send.at[k],
            recv_sem=red_recv.at[k], device_id=t_device(k, -1),
            device_id_type=pl.DeviceIdType.MESH)

    def each(low, high, body):
        def step(k, carry):
            body(k)
            return carry
        lax.fori_loop(low, high, step, 0)

    barrier = pltpu.get_barrier_semaphore()

    def greet(device):
        pl.semaphore_signal(barrier, inc=1, device_id=device,
                            device_id_type=pl.DeviceIdType.MESH)

    loads = [
        pltpu.make_async_copy(a, b, in_sem.at[i])
        for i, (a, b) in enumerate(
            [(level_hbm, level), (pos_hbm, pos), (vel_hbm, vel), (acc_hbm, acc),
             (jerk_hbm, jerk), (mass_hbm, mass), (idx_hbm, idx), (cnt_hbm, cnt)])
    ]
    for load in loads:
        load.start()
    each(1, t, lambda k: greet(t_device(k)))
    near_count = jnp.minimum(hi, NEAR) + jnp.minimum(s - 1 - hi, NEAR)
    each(0, near_count, lambda o: greet((ia, nearest(o) * n_lo + lo)))
    for load in loads:
        load.wait()

    periods = jnp.left_shift(jnp.ones((1, stars), jnp.int32), top_level - level[...])
    remains = jnp.bitwise_and(tick_now, periods - 1)
    age = jnp.where(remains == 0, periods, remains).astype(jnp.float32) * tick_length
    pred_pos = pos[...] + age * (
        vel[...] + age * (acc[...] * 0.5 + age * jerk[...] * (1.0 / 6.0)))
    pred_vel = vel[...] + age * (acc[...] + age * jerk[...] * 0.5)
    src[hi, 0:3] = pred_pos
    src[hi, 3:6] = pred_vel
    src[hi, 6:7] = mass[...]
    src[hi, 7:8] = age

    slot = lax.broadcasted_iota(jnp.int32, (cap, stars), 0)
    want = jnp.zeros((cap, stars), jnp.int32)
    for i in range(cap):
        want = jnp.where(slot == i, idx[i], want)
    mask = lax.broadcasted_iota(jnp.int32, (cap, stars), 1) == want

    def pick(row):
        return jnp.sum(jnp.where(mask, row, 0.0), axis=1, keepdims=True)

    lane = lax.broadcasted_iota(jnp.int32, (cap, LANES), 1)

    def columns(values):
        tile = jnp.zeros((cap, LANES), jnp.float32)
        for i, value in enumerate(values):
            tile = jnp.where(lane == i, value, tile)
        return tile

    own = [pick(src[hi, q:q + 1]) for q in range(6)]
    tgt[0] = columns(own)

    pl.semaphore_wait(barrier, t - 1 + near_count)
    if s == 4:
        @pl.when((hi == 1) | (hi == 2))
        def clear():
            pl.semaphore_signal(ready, inc=1, device_id=(ia, (hi - 1) * 3 * n_lo + lo),
                                device_id_type=pl.DeviceIdType.MESH)
    each(0, near_count, lambda o: src_copy(o).start())
    each(1, t, lambda k: tgt_copy(k).start())
    if s == 4:
        @pl.when((hi == 0) | (hi == 3))
        def far_pair():
            pl.semaphore_wait(ready, 1)
            src_copy(2).start()

    def pairs(k, j, totals):
        tile = tgt[k]
        target = [jnp.broadcast_to(tile[:, q:q + 1], (cap, LANES)) for q in range(6)]
        totals = list(totals)
        for c in range(stars // LANES):
            row = [src[j, q:q + 1, c * LANES:(c + 1) * LANES] for q in range(7)]
            d = [row[q] - target[q] for q in range(3)]
            w = [row[3 + q] - target[3 + q] for q in range(3)]
            u = lax.rsqrt(d[0] * d[0] + d[1] * d[1] + d[2] * d[2] + soft_square)
            u2 = u * u
            m = row[6] * u * u2
            r = 3.0 * (d[0] * w[0] + d[1] * w[1] + d[2] * w[2]) * u2
            for q in range(3):
                totals[q] = totals[q] + m * d[q]
                totals[3 + q] = totals[3 + q] + m * (w[q] - r * d[q])
        return totals

    zeros = [jnp.zeros((cap, LANES), jnp.float32)] * 6

    def add(k, place, totals, last):
        totals = pairs(k, place, totals)
        if last:
            part[k] = columns([jnp.sum(x, axis=1, keepdims=True) for x in totals])
        else:
            for q in range(6):
                sums[k, q] = totals[q]

    add(0, hi, zeros, s == 1)
    old = [pick(acc[q:q + 1, :]) for q in range(3)] + [pick(jerk[q:q + 1, :]) for q in range(3)]
    h = pick(src[hi, 7:8])

    def own_step(k):
        tgt_copy(k).wait_recv()
        add(k, hi, zeros, s == 1)

    each(1, t, own_step)

    for o in range(s - 1):
        src_arrival(o).wait_recv()
        if o < s - 2:
            each(0, t, lambda k: add(k, nearest(o), [sums[k, q] for q in range(6)], False))

    def last_step(i):
        k = (n_ia // 2 + i % n_ia) % n_ia * n_lo + n_lo - 1 - i // n_ia
        if s > 1:
            add(k, nearest(s - 2), [sums[k, q] for q in range(6)], True)

        @pl.when(k != 0)
        def send():
            red_copy(k).start()

    each(0, t, last_step)

    def collect(k, total):
        red_copy(k).wait_recv()
        return total + got[k]

    total = lax.fori_loop(1, t, collect, part[0])
    force = [total[:, q:q + 1] for q in range(6)]
    rows = [None] * 12
    for q in range(3):
        new_acc, new_jerk = force[q], force[3 + q]
        change = old[q] - new_acc
        snap = -6.0 * change - h * (4.0 * old[3 + q] + 2.0 * new_jerk)
        crackle = 12.0 * change + 6.0 * h * (old[3 + q] + new_jerk)
        rows[q] = own[q] + h * h * (snap * (1.0 / 24.0) + crackle * (1.0 / 120.0))
        rows[3 + q] = own[3 + q] + h * (snap * (1.0 / 6.0) + crackle * (1.0 / 24.0))
        rows[6 + q] = new_acc
        rows[9 + q] = new_jerk
    live = lax.broadcasted_iota(jnp.int32, (cap, LANES), 0) < cnt[0]
    result = jnp.where(live, columns(rows), 0.0)
    out_ref[...] = result[:, :12]

    def drain(k):
        tgt_copy(k).wait_send()
        red_copy(k).wait_send()

    each(1, t, drain)
    each(0, s - 1, lambda o: src_copy(o).wait_send())


def on_device(shape, star_pos, star_vel, star_acc, star_jerk, star_mass, star_level,
              active_index, active_count):
    n_ia, n_ja, s = shape
    t = n_ia * (n_ja // s)
    stars = star_mass.shape[0]
    cap = active_index.shape[0]
    f32 = jnp.float32
    return pl.pallas_call(
        functools.partial(kernel, shape),
        out_shape=pltpu.VMEM((cap, 12), f32),
        in_specs=[pl.BlockSpec(memory_space=pltpu.HBM)] * 8,
        out_specs=pl.BlockSpec(memory_space=pltpu.VMEM),
        scratch_shapes=[
            pltpu.VMEM((3, stars), f32), pltpu.VMEM((3, stars), f32),
            pltpu.VMEM((3, stars), f32), pltpu.VMEM((3, stars), f32),
            pltpu.VMEM((1, stars), f32), pltpu.VMEM((1, stars), jnp.int32),
            pltpu.SMEM((cap,), jnp.int32), pltpu.SMEM((1,), jnp.int32),
            pltpu.VMEM((s, 8, stars), f32),
            pltpu.VMEM((t, cap, LANES), f32),
            pltpu.VMEM((t, 6, cap, LANES), f32),
            pltpu.VMEM((t, cap, LANES), f32),
            pltpu.VMEM((t, cap, LANES), f32),
            pltpu.SemaphoreType.DMA((8,)),
            pltpu.SemaphoreType.DMA((s,)), pltpu.SemaphoreType.DMA((s,)),
            pltpu.SemaphoreType.DMA((t,)), pltpu.SemaphoreType.DMA((t,)),
            pltpu.SemaphoreType.DMA((t,)), pltpu.SemaphoreType.DMA((t,)),
            pltpu.SemaphoreType.REGULAR,
        ],
        compiler_params=pltpu.CompilerParams(collective_id=0, has_side_effects=True),
    )(star_pos, star_vel, star_acc, star_jerk, star_mass.reshape(1, stars),
      star_level.reshape(1, stars), active_index, active_count).T


def solution(mesh):
    n_ia, n_ja = mesh.shape["ia"], mesh.shape["ja"]
    s = SOURCE_PARTS if n_ja % SOURCE_PARTS == 0 else 1
    columns = P(None, ("ia", "ja"))
    flat = P(("ia", "ja"))
    return jax.shard_map(
        functools.partial(on_device, (n_ia, n_ja, s)), mesh=mesh,
        in_specs=(columns,) * 4 + (flat,) * 4, out_specs=columns, check_vma=False)
```

```python
import functools

import jax
import jax.numpy as jnp
from jax import lax
from jax.experimental import pallas as pl
from jax.experimental.pallas import tpu as pltpu
from jax.sharding import PartitionSpec as P

tick_now = 44
top_level = 5
tick_length = 0.125
soft_square = 0.0001

LANES = 128
SOURCE_PARTS = 4
NEAR = 2


def kernel(
    shape, pos_hbm, vel_hbm, acc_hbm, jerk_hbm, mass_hbm, level_hbm, idx_hbm, cnt_hbm, out_ref,
    pos, vel, acc, jerk, mass, level, idx, cnt, src, tgt, wide, sums, part, got,
    in_sem, src_send, src_recv, tgt_send, tgt_recv, red_send, red_recv, ready,
):
    n_ia, n_ja, s = shape
    n_lo = n_ja // s
    t = n_ia * n_lo
    stars = pos.shape[1]
    cap = idx.shape[0]
    ia, ja = lax.axis_index("ia"), lax.axis_index("ja")
    hi, lo = ja // n_lo, ja % n_lo

    def t_device(k, sign=1):
        a, b = k // n_lo, k % n_lo
        return ((ia + sign * a + n_ia) % n_ia, hi * n_lo + (lo + sign * b + n_lo) % n_lo)

    def nearest(o):
        up = o + jnp.where(o >= hi, 1, 0)
        down = s - 1 - o - jnp.where(o >= s - 1 - hi, 1, 0)
        return jnp.where(2 * hi < s, up, down)

    def src_copy(o):
        place = nearest(o)
        return pltpu.make_async_remote_copy(
            src_ref=src.at[hi], dst_ref=src.at[hi], send_sem=src_send.at[place],
            recv_sem=src_recv.at[hi], device_id=(ia, place * n_lo + lo),
            device_id_type=pl.DeviceIdType.MESH)

    def src_arrival(o):
        place = nearest(o)
        return pltpu.make_async_remote_copy(
            src_ref=src.at[place], dst_ref=src.at[place], send_sem=src_send.at[place],
            recv_sem=src_recv.at[place], device_id=(ia, place * n_lo + lo),
            device_id_type=pl.DeviceIdType.MESH)

    def tgt_copy(k):
        return pltpu.make_async_remote_copy(
            src_ref=tgt.at[0], dst_ref=tgt.at[k], send_sem=tgt_send.at[k],
            recv_sem=tgt_recv.at[k], device_id=t_device(k),
            device_id_type=pl.DeviceIdType.MESH)

    def red_copy(k):
        return pltpu.make_async_remote_copy(
            src_ref=part.at[k], dst_ref=got.at[k], send_sem=red_send.at[k],
            recv_sem=red_recv.at[k], device_id=t_device(k, -1),
            device_id_type=pl.DeviceIdType.MESH)

    def each(low, high, body):
        def step(k, carry):
            body(k)
            return carry
        lax.fori_loop(low, high, step, 0)

    barrier = pltpu.get_barrier_semaphore()

    def greet(device):
        pl.semaphore_signal(barrier, inc=1, device_id=device,
                            device_id_type=pl.DeviceIdType.MESH)

    loads = [
        pltpu.make_async_copy(a, b, in_sem.at[i])
        for i, (a, b) in enumerate(
            [(level_hbm, level), (pos_hbm, pos), (vel_hbm, vel), (acc_hbm, acc),
             (jerk_hbm, jerk), (mass_hbm, mass), (idx_hbm, idx), (cnt_hbm, cnt)])
    ]
    for load in loads:
        load.start()
    each(1, t, lambda k: greet(t_device(k)))
    near_count = jnp.minimum(hi, NEAR) + jnp.minimum(s - 1 - hi, NEAR)
    each(0, near_count, lambda o: greet((ia, nearest(o) * n_lo + lo)))
    for load in loads:
        load.wait()

    periods = jnp.left_shift(jnp.ones((1, stars), jnp.int32), top_level - level[...])
    remains = jnp.bitwise_and(tick_now, periods - 1)
    age = jnp.where(remains == 0, periods, remains).astype(jnp.float32) * tick_length
    pred_pos = pos[...] + age * (
        vel[...] + age * (acc[...] * 0.5 + age * jerk[...] * (1.0 / 6.0)))
    pred_vel = vel[...] + age * (acc[...] + age * jerk[...] * 0.5)
    src[hi, 0:3] = pred_pos
    src[hi, 3:6] = pred_vel
    src[hi, 6:7] = mass[...]
    src[hi, 7:8] = age

    slot = lax.broadcasted_iota(jnp.int32, (cap, stars), 0)
    want = jnp.zeros((cap, stars), jnp.int32)
    for i in range(cap):
        want = jnp.where(slot == i, idx[i], want)
    mask = lax.broadcasted_iota(jnp.int32, (cap, stars), 1) == want

    def pick(row):
        return jnp.sum(jnp.where(mask, row, 0.0), axis=1, keepdims=True)

    lane = lax.broadcasted_iota(jnp.int32, (cap, LANES), 1)

    def columns(values):
        tile = jnp.zeros((cap, LANES), jnp.float32)
        for i, value in enumerate(values):
            tile = jnp.where(lane == i, value, tile)
        return tile

    own = [pick(src[hi, q:q + 1]) for q in range(6)]
    tgt[0] = columns(own)

    pl.semaphore_wait(barrier, t - 1 + near_count)
    if s == 4:
        @pl.when((hi == 1) | (hi == 2))
        def clear():
            pl.semaphore_signal(ready, inc=1, device_id=(ia, (hi - 1) * 3 * n_lo + lo),
                                device_id_type=pl.DeviceIdType.MESH)
    each(0, near_count, lambda o: src_copy(o).start())
    each(1, t, lambda k: tgt_copy(k).start())
    if s == 4:
        @pl.when((hi == 0) | (hi == 3))
        def far_pair():
            pl.semaphore_wait(ready, 1)
            src_copy(2).start()

    def pairs(target, j, totals):
        totals = list(totals)
        for c in range(stars // LANES):
            row = [src[j, q:q + 1, c * LANES:(c + 1) * LANES] for q in range(7)]
            d = [row[q] - target[q] for q in range(3)]
            w = [row[3 + q] - target[3 + q] for q in range(3)]
            u = lax.rsqrt(d[0] * d[0] + d[1] * d[1] + d[2] * d[2] + soft_square)
            u2 = u * u
            m = row[6] * u * u2
            r = 3.0 * (d[0] * w[0] + d[1] * w[1] + d[2] * w[2]) * u2
            for q in range(3):
                totals[q] = totals[q] + m * d[q]
                totals[3 + q] = totals[3 + q] + m * (w[q] - r * d[q])
        return totals

    zeros = [jnp.zeros((cap, LANES), jnp.float32)] * 6

    size = next(b for b in (4, 2, 1) if t % b == 0)

    def add(i, place, first, last):
        places = [i * size + b for b in range(size)]
        ks = [(n_ia // 2 + p % n_ia) % n_ia * n_lo + n_lo - 1 - p // n_ia for p in places]
        if first:
            tiles = [tgt[k] for k in ks]
            targets = [[jnp.broadcast_to(tile[:, q:q + 1], (cap, LANES)) for q in range(6)]
                       for tile in tiles]
            totals = [zeros] * size
        else:
            targets = [[wide[k, q] for q in range(6)] for k in ks]
            totals = [[sums[k, q] for q in range(6)] for k in ks]
        totals = [pairs(target, place, total) for target, total in zip(targets, totals)]
        if last:
            tiles = [columns([jnp.sum(x, axis=1, keepdims=True) for x in total])
                     for total in totals]
            for k, tile in zip(ks, tiles):
                part[k] = tile
            for k in ks:
                @pl.when(k != 0)
                def send(k=k):
                    red_copy(k).start()
            return
        for k, target, total in zip(ks, targets, totals):
            for q in range(6):
                if first:
                    wide[k, q] = target[q]
                sums[k, q] = total[q]

    old = [pick(acc[q:q + 1, :]) for q in range(3)] + [pick(jerk[q:q + 1, :]) for q in range(3)]
    h = pick(src[hi, 7:8])

    each(1, t, lambda k: tgt_copy(k).wait_recv())
    each(0, t // size, lambda i: add(i, hi, True, s == 1))
    for o in range(s - 1):
        src_arrival(o).wait_recv()
        each(0, t // size, lambda i: add(i, nearest(o), False, o == s - 2))

    def collect(k, total):
        red_copy(k).wait_recv()
        return total + got[k]

    total = lax.fori_loop(1, t, collect, part[0])
    force = [total[:, q:q + 1] for q in range(6)]
    rows = [None] * 12
    for q in range(3):
        new_acc, new_jerk = force[q], force[3 + q]
        change = old[q] - new_acc
        snap = -6.0 * change - h * (4.0 * old[3 + q] + 2.0 * new_jerk)
        crackle = 12.0 * change + 6.0 * h * (old[3 + q] + new_jerk)
        rows[q] = own[q] + h * h * (snap * (1.0 / 24.0) + crackle * (1.0 / 120.0))
        rows[3 + q] = own[3 + q] + h * (snap * (1.0 / 6.0) + crackle * (1.0 / 24.0))
        rows[6 + q] = new_acc
        rows[9 + q] = new_jerk
    live = lax.broadcasted_iota(jnp.int32, (cap, LANES), 0) < cnt[0]
    result = jnp.where(live, columns(rows), 0.0)
    out_ref[...] = result[:, :12]

    def drain(k):
        tgt_copy(k).wait_send()
        red_copy(k).wait_send()

    each(1, t, drain)
    each(0, s - 1, lambda o: src_copy(o).wait_send())


def on_device(shape, star_pos, star_vel, star_acc, star_jerk, star_mass, star_level,
              active_index, active_count):
    n_ia, n_ja, s = shape
    t = n_ia * (n_ja // s)
    stars = star_mass.shape[0]
    cap = active_index.shape[0]
    f32 = jnp.float32
    return pl.pallas_call(
        functools.partial(kernel, shape),
        out_shape=pltpu.VMEM((cap, 12), f32),
        in_specs=[pl.BlockSpec(memory_space=pltpu.HBM)] * 8,
        out_specs=pl.BlockSpec(memory_space=pltpu.VMEM),
        scratch_shapes=[
            pltpu.VMEM((3, stars), f32), pltpu.VMEM((3, stars), f32),
            pltpu.VMEM((3, stars), f32), pltpu.VMEM((3, stars), f32),
            pltpu.VMEM((1, stars), f32), pltpu.VMEM((1, stars), jnp.int32),
            pltpu.SMEM((cap,), jnp.int32), pltpu.SMEM((1,), jnp.int32),
            pltpu.VMEM((s, 8, stars), f32),
            pltpu.VMEM((t, cap, LANES), f32),
            pltpu.VMEM((t, 6, cap, LANES), f32),
            pltpu.VMEM((t, 6, cap, LANES), f32),
            pltpu.VMEM((t, cap, LANES), f32),
            pltpu.VMEM((t, cap, LANES), f32),
            pltpu.SemaphoreType.DMA((8,)),
            pltpu.SemaphoreType.DMA((s,)), pltpu.SemaphoreType.DMA((s,)),
            pltpu.SemaphoreType.DMA((t,)), pltpu.SemaphoreType.DMA((t,)),
            pltpu.SemaphoreType.DMA((t,)), pltpu.SemaphoreType.DMA((t,)),
            pltpu.SemaphoreType.REGULAR,
        ],
        compiler_params=pltpu.CompilerParams(collective_id=0, has_side_effects=True),
    )(star_pos, star_vel, star_acc, star_jerk, star_mass.reshape(1, stars),
      star_level.reshape(1, stars), active_index, active_count).T


def solution(mesh):
    n_ia, n_ja = mesh.shape["ia"], mesh.shape["ja"]
    s = SOURCE_PARTS if n_ja % SOURCE_PARTS == 0 else 1
    columns = P(None, ("ia", "ja"))
    flat = P(("ia", "ja"))
    return jax.shard_map(
        functools.partial(on_device, (n_ia, n_ja, s)), mesh=mesh,
        in_specs=(columns,) * 4 + (flat,) * 4, out_specs=columns, check_vma=False)
```
